512 devices in a mesh: dp: 16 (over y, core), ulysses: 32 (over z, x).
Axes of the slice: x: 4, y: 8, z: 8, core: 2. Of those that a mesh axis runs over, the one named last changes fastest.
Arguments:
- query_rows: bfloat16 [65536, 4096], P(('dp', 'ulysses')), may hold values from -6 to 6
- key_rows: bfloat16 [65536, 512], P(('dp', 'ulysses')), may hold values from -6 to 6
- value_rows: bfloat16 [65536, 512], P(('dp', 'ulysses')), may hold values from -6 to 6
- grad_out: bfloat16 [65536, 4096], P(('dp', 'ulysses')), may hold values from -6 to 6
- doc_lengths: int32 [16, 12], replicated, may hold values from 1 to 2048, 4096 in all within a row
Outputs:
- attention: bfloat16 [65536, 4096], P(('dp', 'ulysses'))
- grad_queries: bfloat16 [65536, 4096], P(('dp', 'ulysses'))
- grad_keys: bfloat16 [65536, 512], P(('dp', 'ulysses'))
- grad_values: bfloat16 [65536, 512], P(('dp', 'ulysses'))
The draws below stay inside these ranges and needn't reach their ends.
Inputs may be any that keep to these rules, and one draw needn't show every extreme that they name: `doc_lengths`: each row's 12 lengths sum to 4096, and the longest is 2048.
All inputs are finite; a program needn't handle non-finite values.
Results may differ from the reference program's by a relative error of at most 0.011.
Values may be sent and summed in bfloat16 or wider, within the bound.
A program may use at most 64 MiB of HBM per device.

```python
import math
import jax
import jax.numpy as jnp
import numpy as np
from jax import lax

HD = 128
DOCS = 12
BLOCK = 512
HQ = 32
KVH = 4
SEQ = 4096
ROWS = 16
MAXDOC = 2048


def draw_query_rows(key, part):
    tokens_all = ROWS * SEQ
    own_key = jax.random.fold_in(key, 3)
    values_now = jnp.clip(jax.random.normal(own_key, (tokens_all, HQ, HD), jnp.float32), -6.0, 6.0)
    return values_now.reshape(tokens_all, HQ * HD).astype(jnp.bfloat16)


def draw_key_rows(key, part):
    tokens_all = ROWS * SEQ
    own_key = jax.random.fold_in(key, 5)
    values_now = jnp.clip(jax.random.normal(own_key, (tokens_all, KVH, HD), jnp.float32), -6.0, 6.0)
    return values_now.reshape(tokens_all, KVH * HD).astype(jnp.bfloat16)


def block_levels(stream_key, extent, pieces, low, high):
    factor_of = 1.0
    for dim, parts in pieces:
        steps = jax.random.uniform(jax.random.fold_in(jax.random.fold_in(stream_key, 6), dim), (parts,), jnp.float32, low / len(pieces), high / len(pieces))
        factor_of = factor_of * jnp.repeat(jnp.exp(steps), extent[dim] // parts).reshape((-1,) + (1,) * (len(extent) - 1 - dim))
    return factor_of


def split_up(amount, total, limit, skew):
    loads = [(1 << 20) // math.isqrt(standing ** skew) + 1 for standing in range(2, amount + 1)]
    spare, holding = total - limit - (amount - 1), [1] * (amount - 1)
    while spare > 0:
        free = [i for i in range(amount - 1) if holding[i] < limit]
        whole, left = sum([loads[i] for i in free]), spare
        for i in free:
            addition = min(limit - holding[i], max(1, left * loads[i] // whole), spare)
            holding[i] = holding[i] + addition
            spare = spare - addition
    return np.array([limit] + holding)


def ragged(rng, number_of, total, bound, slope):
    if number_of == 2:
        one = jax.random.randint(rng, (), max(1, total - bound), min(bound, total - 1) + 1)
        return jnp.stack([one, total - one])
    sizes = jnp.asarray(split_up(number_of, total, bound, slope), jnp.int32)
    couples = (number_of - 1) // 2
    giver, sink = sizes[1:1 + 2 * couples:2], sizes[2:2 + 2 * couples:2]
    margin = jnp.minimum(giver - 1, bound - sink)
    moved = jax.random.randint(jax.random.fold_in(rng, 1), (couples,), 0, 1 << 20) % (margin + 1)
    sizes = sizes.at[1:1 + 2 * couples:2].set(giver - moved).at[2:2 + 2 * couples:2].set(sink + moved)
    return sizes[jax.random.permutation(jax.random.fold_in(rng, 2), number_of)]


def scatter_about(key, dims, deviation, reach, shards=(), kind=jnp.bfloat16):
    drawn = jax.random.normal(key, dims, jnp.float32) * deviation
    if len(shards) > 0:
        drawn = block_levels(key, dims, shards, -0.22, 0.18) * drawn
    return jnp.clip(drawn, min=-reach, max=reach).astype(kind)


def setup_inputs(seed: int = 0) -> dict:
    splits = jax.random.split(jax.random.key(seed), 6)
    query_rows = draw_query_rows(jax.random.fold_in(splits[5], 71), 0)
    key_rows = draw_key_rows(jax.random.fold_in(splits[5], 71), 0)
    value_rows = scatter_about(splits[2], (ROWS * SEQ, KVH * HD), 1.0, 6.0, ((0, 512),))
    grad_out = scatter_about(splits[3], (ROWS * SEQ, HQ * HD), 1.0, 6.0, ((0, 512),))
    doc_lengths = jax.vmap(lambda own: ragged(own, DOCS, SEQ, MAXDOC, 2))(jax.random.split(splits[4], ROWS)).reshape((ROWS, DOCS)).astype(jnp.int32)
    return {"query_rows": query_rows, "key_rows": key_rows, "value_rows": value_rows, "grad_out": grad_out, "doc_lengths": doc_lengths}


masked_score = -1e+30

def doc_starts(row_lengths, length):
    doc_ends = jnp.cumsum(row_lengths).astype(jnp.int32)
    positions = jnp.arange(length, dtype=jnp.int32)
    passed = (doc_ends[None, :] <= positions[:, None]).astype(jnp.int32)
    return lax.optimization_barrier(jnp.sum(passed * row_lengths[None, :], axis=1)).astype(jnp.int32)

def attend_head(query_head, key_head, value_head, grad_head, starts, owned_blocks, block_rows):
    length, head_width = query_head.shape
    blocks = length // block_rows
    score_scale = 1.0 / math.sqrt(head_width)
    offsets = jnp.arange(block_rows, dtype=jnp.int32)
    block_first = starts.reshape(blocks, block_rows)[:, 0]

    def forward_block(query_index, carried):
        output_rows, log_totals = carried
        row_start = query_index * block_rows
        query_block = lax.dynamic_slice_in_dim(query_head, row_start, block_rows, 0)
        first_key = lax.dynamic_slice_in_dim(starts, row_start, block_rows, 0)
        query_pos = row_start + offsets

        def key_step(key_index, status):
            key_start = key_index * block_rows
            needed = owned_blocks[query_index] & (key_start + block_rows - 1 >= block_first[query_index])

            def update(status):
                running_max, running_sum, totals = status
                key_block = lax.dynamic_slice_in_dim(key_head, key_start, block_rows, 0)
                value_block = lax.dynamic_slice_in_dim(value_head, key_start, block_rows, 0)
                key_pos = key_start + offsets
                allowed = (key_pos[None, :] <= query_pos[:, None]) & (key_pos[None, :] >= first_key[:, None])
                scores = jnp.dot(query_block, key_block.T, preferred_element_type=jnp.float32) * score_scale
                scores = jnp.where(allowed, scores, masked_score)
                new_max = jnp.maximum(running_max, lax.optimization_barrier(jnp.max(scores, axis=1)))
                weights = jnp.where(allowed, jnp.exp(scores - new_max[:, None]), 0.0)
                factor = jnp.exp(running_max - new_max)
                running_sum = running_sum * factor + lax.optimization_barrier(jnp.sum(weights, axis=1))
                totals = totals * factor[:, None] + jnp.dot(weights.astype(jnp.bfloat16), value_block, preferred_element_type=jnp.float32)
                return (new_max, running_sum, totals)
            return lax.cond(needed, update, lambda unchanged: unchanged, status)
        start_status = (jnp.full((block_rows,), masked_score, dtype=jnp.float32), jnp.zeros((block_rows,), jnp.float32), jnp.zeros((block_rows, head_width), jnp.float32))
        running_max, running_sum, totals = lax.fori_loop(0, query_index + 1, key_step, start_status)
        safe_sum = jnp.where(owned_blocks[query_index], running_sum, 1.0)
        output_block = (totals / safe_sum[:, None]).astype(jnp.bfloat16)
        output_rows = lax.dynamic_update_slice_in_dim(output_rows, output_block, row_start, 0)
        log_totals = lax.dynamic_update_slice_in_dim(log_totals, running_max + jnp.log(safe_sum), row_start, 0)
        return (output_rows, log_totals)
    output_rows, log_totals = lax.fori_loop(0, blocks, forward_block, (jnp.zeros((length, head_width), jnp.bfloat16), jnp.zeros((length,), jnp.float32)))
    row_dots = lax.optimization_barrier(jnp.sum(grad_head.astype(jnp.float32) * output_rows.astype(jnp.float32), axis=1))

    def backward_block(key_index, carried):
        grad_query, grad_key, grad_value = carried
        key_start = key_index * block_rows
        key_block = lax.dynamic_slice_in_dim(key_head, key_start, block_rows, 0)
        value_block = lax.dynamic_slice_in_dim(value_head, key_start, block_rows, 0)
        key_pos = key_start + offsets

        def query_step(query_index, status):
            row_start = query_index * block_rows
            needed = owned_blocks[query_index] & (key_start + block_rows - 1 >= block_first[query_index])

            def update(status):
                query_sum, key_sum, value_sum = status
                query_block = lax.dynamic_slice_in_dim(query_head, row_start, block_rows, 0)
                grad_block = lax.dynamic_slice_in_dim(grad_head, row_start, block_rows, 0)
                log_block = lax.dynamic_slice_in_dim(log_totals, row_start, block_rows, 0)
                dot_block = lax.dynamic_slice_in_dim(row_dots, row_start, block_rows, 0)
                first_key = lax.dynamic_slice_in_dim(starts, row_start, block_rows, 0)
                query_pos = row_start + offsets
                allowed = (key_pos[None, :] <= query_pos[:, None]) & (key_pos[None, :] >= first_key[:, None])
                scores = jnp.dot(query_block, key_block.T, preferred_element_type=jnp.float32) * score_scale
                weights = jnp.where(allowed, jnp.exp(scores - log_block[:, None]), 0.0)
                weights_low = weights.astype(jnp.bfloat16)
                value_sum = value_sum + jnp.dot(weights_low.T, grad_block, preferred_element_type=jnp.float32)
                grad_weights = jnp.dot(grad_block, value_block.T, preferred_element_type=jnp.float32)
                grad_scores = (weights * (grad_weights - dot_block[:, None])).astype(jnp.bfloat16)
                key_sum = key_sum + jnp.dot(grad_scores.T, query_block, preferred_element_type=jnp.float32) * score_scale
                query_now = lax.dynamic_slice_in_dim(query_sum, row_start, block_rows, 0) + jnp.dot(grad_scores, key_block, preferred_element_type=jnp.float32) * score_scale
                query_sum = lax.dynamic_update_slice_in_dim(query_sum, query_now, row_start, 0)
                return (query_sum, key_sum, value_sum)
            return lax.cond(needed, update, lambda unchanged: unchanged, status)
        zeros_block = jnp.zeros((block_rows, head_width), jnp.float32)
        grad_query, key_sum, value_sum = lax.fori_loop(key_index, blocks, query_step, (grad_query, zeros_block, zeros_block))
        grad_key = lax.dynamic_update_slice_in_dim(grad_key, key_sum, key_start, 0)
        grad_value = lax.dynamic_update_slice_in_dim(grad_value, value_sum, key_start, 0)
        return (grad_query, grad_key, grad_value)
    zero_rows = jnp.zeros((length, head_width), jnp.float32)
    grad_query, grad_key, grad_value = lax.fori_loop(0, blocks, backward_block, (zero_rows, zero_rows, zero_rows))
    return (output_rows, grad_query.astype(jnp.bfloat16), grad_key, grad_value)

def reference(query_rows, key_rows, value_rows, grad_out, doc_lengths):
    row_count = doc_lengths.shape[0]
    length = query_rows.shape[0] // row_count
    query_heads = query_rows.shape[1] // HD
    shared_heads = key_rows.shape[1] // HD
    group_size = query_heads // shared_heads
    queries = query_rows.reshape(row_count, length, query_heads, HD)
    key_split = key_rows.reshape(row_count, length, shared_heads, HD)
    value_split = value_rows.reshape(row_count, length, shared_heads, HD)
    grad_split = grad_out.reshape(row_count, length, query_heads, HD)
    owned_blocks = jnp.ones((length // BLOCK,), dtype=bool)

    def one_group(position):
        row_index = position // shared_heads
        shared = position % shared_heads
        starts = doc_starts(doc_lengths[row_index], length)
        key_head = key_split[row_index, :, shared]
        value_head = value_split[row_index, :, shared]

        def one_head(member):
            head_index = shared * group_size + member
            result = attend_head(queries[row_index, :, head_index], key_head, value_head, grad_split[row_index, :, head_index], starts, owned_blocks, BLOCK)
            return (result[0], result[1], result[2].astype(jnp.bfloat16), result[3].astype(jnp.bfloat16))
        outputs, grad_query, key_terms, value_terms = lax.map(one_head, jnp.arange(group_size, dtype=jnp.int32))
        grad_key = lax.optimization_barrier(jnp.sum(key_terms.astype(jnp.float32), axis=0)).astype(jnp.bfloat16)
        grad_value = lax.optimization_barrier(jnp.sum(value_terms.astype(jnp.float32), axis=0)).astype(jnp.bfloat16)
        return (outputs, grad_query, grad_key, grad_value)
    outputs, grad_query, grad_key, grad_value = lax.map(one_group, jnp.arange(row_count * shared_heads, dtype=jnp.int32))
    attention = outputs.reshape(row_count, shared_heads, group_size, length, HD).transpose(0, 3, 1, 2, 4).reshape(row_count * length, query_heads * HD)
    grad_queries = grad_query.reshape(row_count, shared_heads, group_size, length, HD).transpose(0, 3, 1, 2, 4).reshape(row_count * length, query_heads * HD)
    grad_keys = grad_key.reshape(row_count, shared_heads, length, HD).transpose(0, 2, 1, 3).reshape(row_count * length, shared_heads * HD)
    grad_values = grad_value.reshape(row_count, shared_heads, length, HD).transpose(0, 2, 1, 3).reshape(row_count * length, shared_heads * HD)
    return (attention, grad_queries, grad_keys, grad_values)
```

```python
import math

import jax
import jax.numpy as jnp
from jax import lax
from jax.experimental import pallas as pl
from jax.experimental.pallas import tpu as pltpu
from jax.sharding import PartitionSpec as P

HD = 128
XS = 4
ZS = 8
SH = 128
BLK = XS * SH
NB = 5
GRP = 8
DOCS = 12
HALF = 256
SCALE = 1.0 / math.sqrt(HD)
LOG2 = SCALE * math.log2(math.e)
BIG = -(2.0**100)
MESH = pl.DeviceIdType.MESH
F32 = jnp.float32
BF16 = jnp.bfloat16


def dot(a, b):
    return jnp.dot(a, b, preferred_element_type=F32)


def aligned(index, size):
    return pl.ds(pl.multiple_of(index * size, size), size)


def query_range(b, c):
    if b == NB - 1:
        return (0, BLK) if c < 2 else (HALF, BLK)
    if b == 0:
        return (0, HALF) if c < 2 else (0, BLK)
    return (0, BLK)


def backward_tiles(b):
    if b == NB - 1:
        return [(0, HALF, 0, BLK), (HALF, HALF, HALF, HALF)]
    if b == 0:
        return [(0, HALF, 0, HALF), (HALF, HALF, 0, BLK)]
    return [(0, BLK, 0, BLK)]


def kernel(
    dl, q_in, k_in, v_in, g_in,
    att, dq_out, dk_out, dv_out,
    kw, vw, qn, gn, on, dqn,
    qx, gT, kx, kT, vTx, prob, acc, maxes, sums, dqT, scal, s_a, s_b,
    dkv, dkv_own, ring_in, ring_out, last,
    in_send, in_recv, loc, hop_send, hop_recv, o_send, o_recv, dq_send, dq_recv,
    red_send, red_recv, fin_send, fin_recv,
):
    dp = lax.axis_index("dp")
    u = lax.axis_index("ulysses")
    x = lax.rem(u, XS)
    z = lax.div(u, XS)
    peer_x = [lax.rem(x + r, XS) for r in range(XS)]
    peers = [(dp, z * XS + peer_x[r]) for r in range(XS)]
    up = (dp, lax.rem(z + 1, ZS) * XS + x)
    down = (dp, lax.rem(z + ZS - 1, ZS) * XS + x)

    def remote(src, dst, send, recv, device):
        return pltpu.make_async_remote_copy(
            src_ref=src, dst_ref=dst, send_sem=send, recv_sem=recv,
            device_id=device, device_id_type=MESH,
        )

    barrier = pltpu.get_barrier_semaphore()
    for device in (peers[1], peers[2], peers[3], up, down):
        pl.semaphore_signal(barrier, inc=1, device_id=device, device_id_type=MESH)
    pl.semaphore_wait(barrier, 5)

    mine = aligned(x, SH)
    wide = GRP * HD
    moves = (
        (k_in, HD, kw.at[NB - 1]),
        (v_in, HD, vw.at[NB - 1]),
        (q_in, wide, qn),
        (g_in, wide, gn),
    )
    arrive = []
    local = []
    for n, (src, width, dst) in enumerate(moves):
        row = []
        for r in (1, 3, 2):
            copy = remote(
                src.at[:, aligned(peer_x[r], width)], dst.at[mine, :],
                in_send.at[n, r], in_recv.at[n, r], peers[r],
            )
            copy.start()
            row.append(copy)
        own = pltpu.make_async_copy(src.at[:, aligned(x, width)], dst.at[mine, :], loc.at[n])
        own.start()
        arrive.append(row)
        local.append(own)

    def arrived(n):
        local[n].wait()
        for copy in arrive[n]:
            copy.wait()

    hops = {}

    def hop(b):
        hops[b] = [
            remote(w.at[b], w.at[b - 1], hop_send.at[n, b], hop_recv.at[n, b], up)
            for n, w in enumerate((kw, vw))
        ]
        for copy in hops[b]:
            copy.start()

    def hopped(b):
        for copy in hops[b]:
            copy.wait()

    base = (z - (NB - 1)) * BLK
    lane = lax.broadcasted_iota(jnp.int32, (1, HD), 1)
    key_lo = jnp.full((1, HD), 1 << 30, jnp.int32)
    key_hi = jnp.full((1, HD), -(1 << 30), jnp.int32)
    sub = lax.broadcasted_iota(jnp.int32, (HD, BLK), 0)
    pos = lax.broadcasted_iota(jnp.int32, (HD, BLK), 1) + (NB - 1) * BLK
    bias = jnp.where(sub == DOCS, BIG, 0.0).astype(F32)
    first = -base
    for d in range(DOCS):
        end = first + dl[dp, d]
        key_lo = jnp.where(lane == d, first, key_lo)
        key_hi = jnp.where(lane == d, end, key_hi)
        inside = (pos >= first) & (pos < end)
        bias = jnp.where((sub == d) & jnp.logical_not(inside), BIG, bias)
        first = end
    key_lo = jnp.where(lane == DOCS, -(1 << 30), key_lo)
    key_hi = jnp.where(lane == DOCS, -base, key_hi)
    bias = bias.astype(BF16)
    for h in range(GRP):
        qx[h, HD:, :] = bias

    def prepare(b):
        j = lax.broadcasted_iota(jnp.int32, (BLK, HD), 0) + b * BLK
        kx[b, :, HD:] = jnp.where((j >= key_lo) & (j < key_hi), 1.0, 0.0).astype(BF16)
        kx[b, :, 0:HD] = kw[b]
        kT[b] = kw[b].T
        vTx[b, 0:HD, :] = vw[b].T
        vTx[b, HD:, :] = jnp.ones((16, BLK), BF16)

    def scores(b, h, to, c, tops):
        q0, q1 = query_range(b, c)
        rows = slice(c * SH, c * SH + SH)
        s = dot(kx[b, rows, :], qx[h, :, q0:q1])
        if b == NB - 1:
            j = lax.broadcasted_iota(jnp.int32, (SH, q1 - q0), 0) + c * SH
            i = lax.broadcasted_iota(jnp.int32, (SH, q1 - q0), 1) + q0
            s = jnp.where(j <= i, s, BIG)
        to[rows, q0:q1] = s
        top = jnp.max(s, axis=0, keepdims=True)
        for n, lo in enumerate((0, HALF)):
            if q0 <= lo and lo + HALF <= q1:
                t = top[:, lo - q0 : lo - q0 + HALF]
                tops[n] = t if tops[n] is None else jnp.maximum(tops[n], t)

    def put_tops(b, h, tops):
        for n in range(2):
            maxes[h, b : b + 1, n * HALF : n * HALF + HALF] = tops[n]

    def forward(b):
        tops = [None, None]
        for c in range(4):
            scores(b, 0, s_a, c, tops)
        put_tops(b, 0, tops)

        def one(h, now, later):
            ahead = jnp.minimum(h + 1, GRP - 1)
            top = maxes[h, b : b + 1, :]
            tops = [None, None]
            outs = [None, None]
            held = None
            for c in range(4):
                scores(b, ahead, later, c, tops)
                q0, q1 = query_range(b, c)
                rows = slice(c * SH, c * SH + SH)
                p = jnp.exp2((now[rows, q0:q1] - top[:, q0:q1]) * LOG2).astype(BF16)
                prob[h, b, rows, q0:q1] = p
                if c % 2:
                    pair = jnp.concatenate([held, p], axis=0)
                    t = dot(vTx[b, :, c * SH - SH : c * SH + SH], pair)
                    for n, lo in enumerate((0, HALF)):
                        if q0 <= lo and lo + HALF <= q1:
                            part = t[:, lo - q0 : lo - q0 + HALF]
                            outs[n] = part if outs[n] is None else outs[n] + part
                held = p
            put_tops(b, ahead, tops)
            for n in range(2):
                qs = slice(n * HALF, n * HALF + HALF)
                out, total, peak = outs[n][0:HD], outs[n][HD : HD + 1], top[:, qs]
                if b == NB - 1:
                    maxes[h, NB : NB + 1, qs] = peak
                    sums[h, 0:1, qs] = total
                    acc[h, :, qs] = out
                else:
                    old = maxes[h, NB : NB + 1, qs]
                    new = jnp.maximum(old, peak)
                    keep = jnp.exp2((old - new) * LOG2)
                    add = jnp.exp2((peak - new) * LOG2)
                    maxes[h, NB : NB + 1, qs] = new
                    sums[h, 0:1, qs] = sums[h, 0:1, qs] * keep + total * add
                    acc[h, :, qs] = acc[h, :, qs] * keep + out * add

        def two(pair, _):
            one(pair * 2, s_a, s_b)
            one(pair * 2 + 1, s_b, s_a)
            return 0

        lax.fori_loop(0, GRP // 2, two, 0)

    def backward(b, h, into):
        cols = aligned(h, HD)
        for n, (k0, kl, q0, ql) in enumerate(backward_tiles(b)):
            ks, qs = slice(k0, k0 + kl), slice(q0, q0 + ql)
            w = prob[h, b, ks, qs].astype(F32) * scal[h, b : b + 1, qs]
            gw = dot(vw[b, ks, :], gT[h, :, qs])
            gs = (w * (gw - scal[h, NB : NB + 1, qs])).astype(BF16)
            low = w.astype(BF16)
            into[1, ks, :] += dot(low, gn[qs, cols])
            into[0, ks, :] += dot(gs, qn[qs, cols])
            t = dot(kT[b, :, ks], gs)
            if b == 0 and n == 0:
                dqT[h, :, qs] = t
                dqT[h, :, HALF:] = jnp.zeros((HD, HALF), F32)
            else:
                dqT[h, :, qs] += t
        if b == NB - 1:
            dqn[:, cols] = (dqT[h] * SCALE).astype(BF16).T

    arrived(0)
    arrived(1)
    hop(4)
    prepare(4)
    hopped(4)
    hop(3)
    prepare(3)
    arrived(2)
    for h in range(GRP):
        qx[h, 0:HD, :] = qn[:, h * HD : h * HD + HD].T
    forward(4)
    hopped(3)
    hop(2)
    forward(3)
    prepare(2)
    hopped(2)
    hop(1)
    forward(2)
    prepare(1)
    forward(1)
    hopped(1)
    prepare(0)
    forward(0)

    arrived(3)
    for h in range(GRP):
        gT[h] = gn[:, h * HD : h * HD + HD].T

    def finish(h, _):
        inv = 1.0 / sums[h, 0:1, :]
        o = (acc[h] * inv).astype(BF16)
        scal[h, NB : NB + 1, :] = jnp.sum(
            o.astype(F32) * gT[h].astype(F32), axis=0, keepdims=True
        )
        for b in range(NB):
            scal[h, b : b + 1, :] = (
                jnp.exp2((maxes[h, b : b + 1, :] - maxes[h, NB : NB + 1, :]) * LOG2) * inv
            )
        on[:, aligned(h, HD)] = o.T
        return 0

    lax.fori_loop(0, GRP, finish, 0)

    slab = aligned(x, wide)
    tail = []
    for r in (1, 3, 2):
        copy = remote(
            on.at[aligned(peer_x[r], SH), :], att.at[:, slab], o_send.at[r], o_recv.at[r], peers[r]
        )
        copy.start()
        tail.append(copy)
    own = pltpu.make_async_copy(on.at[mine, :], att.at[:, slab], loc.at[4])
    own.start()
    tail.append(own)

    def pass_on(b):
        for n in range(2):
            total = dkv[n] * SCALE if n == 0 else dkv[n]
            if b > 0:
                reds[n, b - 1].wait()
                total = total + ring_in[b - 1, n].astype(F32)
            ring_out[b, n] = total.astype(BF16)
            reds[n, b] = remote(
                ring_out.at[b, n], ring_in.at[b, n], red_send.at[n, b], red_recv.at[n, b], down
            )
            reds[n, b].start()

    reds = {}
    for b in range(3):
        dkv[...] = jnp.zeros((2, BLK, HD), F32)

        def step(h, _, b=b):
            backward(b, h, dkv)
            return 0

        lax.fori_loop(0, GRP, step, 0)
        pass_on(b)
    dkv[...] = jnp.zeros((2, BLK, HD), F32)
    dkv_own[...] = jnp.zeros((2, BLK, HD), F32)
    part = wide // 2
    for half in range(2):
        first_head = half * (GRP // 2)

        def near(h, _):
            backward(3, h, dkv)
            return 0

        lax.fori_loop(first_head, first_head + GRP // 2, near, 0)
        if half == 1:
            pass_on(3)

        def nearest(h, _):
            backward(4, h, dkv_own)
            return 0

        lax.fori_loop(first_head, first_head + GRP // 2, nearest, 0)
        here = pl.ds(half * part, part)
        there = pl.ds(pl.multiple_of(x * wide + half * part, part), part)
        for r in (1, 3, 2):
            copy = remote(
                dqn.at[aligned(peer_x[r], SH), here], dq_out.at[:, there],
                dq_send.at[half, r], dq_recv.at[half, r], peers[r],
            )
            copy.start()
            tail.append(copy)
        own = pltpu.make_async_copy(dqn.at[mine, here], dq_out.at[:, there], loc.at[5 + half])
        own.start()
        tail.append(own)

    heads = aligned(x, HD)
    for n, out in enumerate((dk_out, dv_out)):
        total = dkv_own[n] * SCALE if n == 0 else dkv_own[n]
        reds[n, 3].wait()
        last[n] = (total + ring_in[3, n].astype(F32)).astype(BF16)
        for r in (1, 3, 2):
            copy = remote(
                last.at[n, aligned(peer_x[r], SH), :], out.at[:, heads],
                fin_send.at[n, r], fin_recv.at[n, r], peers[r],
            )
            copy.start()
            tail.append(copy)
        own = pltpu.make_async_copy(last.at[n, mine, :], out.at[:, heads], loc.at[7 + n])
        own.start()
        tail.append(own)
    for copy in tail:
        copy.wait()


def per_device(query_rows, key_rows, value_rows, grad_out, doc_lengths):
    anywhere = pl.BlockSpec(memory_space=pl.ANY)
    dma = pltpu.SemaphoreType.DMA
    wide = GRP * HD
    shapes = [query_rows.shape, query_rows.shape, key_rows.shape, value_rows.shape]
    return pl.pallas_call(
        kernel,
        out_shape=[jax.ShapeDtypeStruct(s, BF16) for s in shapes],
        in_specs=[pl.BlockSpec(memory_space=pltpu.SMEM)] + [anywhere] * 4,
        out_specs=[anywhere] * 4,
        scratch_shapes=[
            pltpu.VMEM((NB, BLK, HD), BF16),
            pltpu.VMEM((NB, BLK, HD), BF16),
            pltpu.VMEM((BLK, wide), BF16),
            pltpu.VMEM((BLK, wide), BF16),
            pltpu.VMEM((BLK, wide), BF16),
            pltpu.VMEM((BLK, wide), BF16),
            pltpu.VMEM((GRP, 2 * HD, BLK), BF16),
            pltpu.VMEM((GRP, HD, BLK), BF16),
            pltpu.VMEM((NB, BLK, 2 * HD), BF16),
            pltpu.VMEM((NB, HD, BLK), BF16),
            pltpu.VMEM((NB, HD + 16, BLK), BF16),
            pltpu.VMEM((GRP, NB, BLK, BLK), BF16),
            pltpu.VMEM((GRP, HD, BLK), F32),
            pltpu.VMEM((GRP, 8, BLK), F32),
            pltpu.VMEM((GRP, 8, BLK), F32),
            pltpu.VMEM((GRP, HD, BLK), F32),
            pltpu.VMEM((GRP, 8, BLK), F32),
            pltpu.VMEM((BLK, BLK), F32),
            pltpu.VMEM((BLK, BLK), F32),
            pltpu.VMEM((2, BLK, HD), F32),
            pltpu.VMEM((2, BLK, HD), F32),
            pltpu.VMEM((4, 2, BLK, HD), BF16),
            pltpu.VMEM((4, 2, BLK, HD), BF16),
            pltpu.VMEM((2, BLK, HD), BF16),
            dma((4, 4)),
            dma((4, 4)),
            dma((9,)),
            dma((2, 5)),
            dma((2, 5)),
            dma((4,)),
            dma((4,)),
            dma((2, 4)),
            dma((2, 4)),
            dma((2, 4)),
            dma((2, 4)),
            dma((2, 4)),
            dma((2, 4)),
        ],
        compiler_params=pltpu.CompilerParams(
            collective_id=0, has_side_effects=True, vmem_limit_bytes=60 * 1024 * 1024
        ),
    )(doc_lengths, query_rows, key_rows, value_rows, grad_out)


def solution(mesh):
    rows = P(("dp", "ulysses"), None)
    return jax.shard_map(
        per_device,
        mesh=mesh,
        in_specs=(rows, rows, rows, rows, P()),
        out_specs=(rows, rows, rows, rows),
        check_vma=False,
    )
```

```python
import math

import jax
import jax.numpy as jnp
from jax import lax
from jax.experimental import pallas as pl
from jax.experimental.pallas import tpu as pltpu
from jax.sharding import PartitionSpec as P

HD = 128
XS = 4
ZS = 8
SH = 128
BLK = XS * SH
NB = 5
GRP = 8
DOCS = 12
HALF = 256
SCALE = 1.0 / math.sqrt(HD)
LOG2 = SCALE * math.log2(math.e)
BIG = -(2.0**100)
MESH = pl.DeviceIdType.MESH
F32 = jnp.float32
BF16 = jnp.bfloat16


def dot(a, b):
    return jnp.dot(a, b, preferred_element_type=F32)


def aligned(index, size):
    return pl.ds(pl.multiple_of(index * size, size), size)


def query_range(b, c):
    if b == NB - 1:
        return (0, BLK) if c < 2 else (HALF, BLK)
    if b == 0:
        return (0, HALF) if c < 2 else (0, BLK)
    return (0, BLK)


def backward_tiles(b):
    if b == NB - 1:
        return [(0, HALF, 0, BLK), (HALF, HALF, HALF, HALF)]
    if b == 0:
        return [(0, HALF, 0, HALF), (HALF, HALF, 0, BLK)]
    return [(0, BLK, 0, BLK)]


def kernel(
    dl, q_in, k_in, v_in, g_in,
    att, dq_out, dk_out, dv_out,
    kw, vw, qn, gn, on, dqn,
    qx, gT, kx, kT, vTx, prob, acc, maxes, sums, dqT, scal, s_a, s_b,
    dkv, dkv_own, ring_in, ring_out, last,
    in_send, in_recv, loc, hop_send, hop_recv, o_send, o_recv, dq_send, dq_recv, dq_loc,
    red_send, red_recv, fin_send, fin_recv,
):
    dp = lax.axis_index("dp")
    u = lax.axis_index("ulysses")
    x = lax.rem(u, XS)
    z = lax.div(u, XS)
    peer_x = [lax.rem(x + r, XS) for r in range(XS)]
    peers = [(dp, z * XS + peer_x[r]) for r in range(XS)]
    up = (dp, lax.rem(z + 1, ZS) * XS + x)
    down = (dp, lax.rem(z + ZS - 1, ZS) * XS + x)

    def remote(src, dst, send, recv, device):
        return pltpu.make_async_remote_copy(
            src_ref=src, dst_ref=dst, send_sem=send, recv_sem=recv,
            device_id=device, device_id_type=MESH,
        )

    barrier = pltpu.get_barrier_semaphore()
    for device in (peers[1], peers[2], peers[3], up, down):
        pl.semaphore_signal(barrier, inc=1, device_id=device, device_id_type=MESH)
    pl.semaphore_wait(barrier, 5)

    mine = aligned(x, SH)
    wide = GRP * HD
    part = wide // 2
    moves = (
        (k_in, HD, 0, HD, kw.at[NB - 1]),
        (v_in, HD, 0, HD, vw.at[NB - 1]),
        (q_in, wide, 0, part, qn),
        (q_in, wide, part, part, qn),
        (g_in, wide, 0, wide, gn),
    )
    arrive = []
    local = []
    for n, (src, step_by, skip, width, dst) in enumerate(moves):
        row = []
        into = dst.at[mine, pl.ds(skip, width)]
        for r in (1, 3, 2):
            cols = pl.ds(pl.multiple_of(peer_x[r] * step_by + skip, HD), width)
            copy = remote(src.at[:, cols], into, in_send.at[n, r], in_recv.at[n, r], peers[r])
            copy.start()
            row.append(copy)
        cols = pl.ds(pl.multiple_of(x * step_by + skip, HD), width)
        own = pltpu.make_async_copy(src.at[:, cols], into, loc.at[n])
        own.start()
        arrive.append(row)
        local.append(own)

    def arrived(n):
        local[n].wait()
        for copy in arrive[n]:
            copy.wait()

    hops = {}

    windows = (kw, vw)

    def hop(n, b):
        w = windows[n]
        hops[n, b] = remote(w.at[b], w.at[b - 1], hop_send.at[n, b], hop_recv.at[n, b], up)
        hops[n, b].start()

    def relay(n, b):
        hops[n, b + 1].wait()
        if b > 0:
            hop(n, b)

    base = (z - (NB - 1)) * BLK
    lane = lax.broadcasted_iota(jnp.int32, (1, HD), 1)
    key_lo = jnp.full((1, HD), 1 << 30, jnp.int32)
    key_hi = jnp.full((1, HD), -(1 << 30), jnp.int32)
    sub = lax.broadcasted_iota(jnp.int32, (HD, BLK), 0)
    pos = lax.broadcasted_iota(jnp.int32, (HD, BLK), 1) + (NB - 1) * BLK
    bias = jnp.where(sub == DOCS, BIG, 0.0).astype(F32)
    first = -base
    for d in range(DOCS):
        end = first + dl[dp, d]
        key_lo = jnp.where(lane == d, first, key_lo)
        key_hi = jnp.where(lane == d, end, key_hi)
        inside = (pos >= first) & (pos < end)
        bias = jnp.where((sub == d) & jnp.logical_not(inside), BIG, bias)
        first = end
    key_lo = jnp.where(lane == DOCS, -(1 << 30), key_lo)
    key_hi = jnp.where(lane == DOCS, -base, key_hi)
    bias = bias.astype(BF16)
    for h in range(GRP):
        qx[h, HD:, :] = bias

    def prepare_keys(b):
        j = lax.broadcasted_iota(jnp.int32, (BLK, HD), 0) + b * BLK
        kx[b, :, HD:] = jnp.where((j >= key_lo) & (j < key_hi), 1.0, 0.0).astype(BF16)
        kx[b, :, 0:HD] = kw[b]
        kT[b] = kw[b].T

    def prepare_values(b):
        vTx[b, 0:HD, :] = vw[b].T
        vTx[b, HD:, :] = jnp.ones((16, BLK), BF16)

    def scores(b, h, to, c, tops):
        q0, q1 = query_range(b, c)
        rows = slice(c * SH, c * SH + SH)
        s = dot(kx[b, rows, :], qx[h, :, q0:q1])
        if b == NB - 1:
            j = lax.broadcasted_iota(jnp.int32, (SH, q1 - q0), 0) + c * SH
            i = lax.broadcasted_iota(jnp.int32, (SH, q1 - q0), 1) + q0
            s = jnp.where(j <= i, s, BIG)
        to[rows, q0:q1] = s
        top = jnp.max(s, axis=0, keepdims=True)
        for n, lo in enumerate((0, HALF)):
            if q0 <= lo and lo + HALF <= q1:
                t = top[:, lo - q0 : lo - q0 + HALF]
                tops[n] = t if tops[n] is None else jnp.maximum(tops[n], t)

    def put_tops(b, h, tops):
        for n in range(2):
            maxes[h, b : b + 1, n * HALF : n * HALF + HALF] = tops[n]

    def forward(b, h, now, later, ahead):
        top = maxes[h, b : b + 1, :]
        tops = [None, None]
        outs = [None, None]
        held = None
        for c in range(4):
            if ahead is not None:
                scores(*ahead, later, c, tops)
            q0, q1 = query_range(b, c)
            rows = slice(c * SH, c * SH + SH)
            p = jnp.exp2((now[rows, q0:q1] - top[:, q0:q1]) * LOG2).astype(BF16)
            prob[h, b, rows, q0:q1] = p
            if c % 2:
                pair = jnp.concatenate([held, p], axis=0)
                t = dot(vTx[b, :, c * SH - SH : c * SH + SH], pair)
                for n, lo in enumerate((0, HALF)):
                    if q0 <= lo and lo + HALF <= q1:
                        piece = t[:, lo - q0 : lo - q0 + HALF]
                        outs[n] = piece if outs[n] is None else outs[n] + piece
            held = p
        if ahead is not None:
            put_tops(*ahead, tops)
        for n in range(2):
            qs = slice(n * HALF, n * HALF + HALF)
            out, total, peak = outs[n][0:HD], outs[n][HD : HD + 1], top[:, qs]
            if b == NB - 1:
                maxes[h, NB : NB + 1, qs] = peak
                sums[h, 0:1, qs] = total
                acc[h, :, qs] = out
            else:
                old = maxes[h, NB : NB + 1, qs]
                new = jnp.maximum(old, peak)
                keep = jnp.exp2((old - new) * LOG2)
                add = jnp.exp2((peak - new) * LOG2)
                maxes[h, NB : NB + 1, qs] = new
                sums[h, 0:1, qs] = sums[h, 0:1, qs] * keep + total * add
                acc[h, :, qs] = acc[h, :, qs] * keep + out * add

    def backward(b, h, into):
        cols = aligned(h, HD)
        for n, (k0, kl, q0, ql) in enumerate(backward_tiles(b)):
            ks, qs = slice(k0, k0 + kl), slice(q0, q0 + ql)
            w = prob[h, b, ks, qs].astype(F32) * scal[h, b : b + 1, qs]
            gw = dot(vw[b, ks, :], gT[h, :, qs])
            gs = (w * (gw - scal[h, NB : NB + 1, qs])).astype(BF16)
            low = w.astype(BF16)
            into[1, ks, :] += dot(low, gn[qs, cols])
            into[0, ks, :] += dot(gs, qn[qs, cols])
            t = dot(kT[b, :, ks], gs)
            if b == 0 and n == 0:
                dqT[h, :, qs] = t
                dqT[h, :, HALF:] = jnp.zeros((HD, HALF), F32)
            else:
                dqT[h, :, qs] += t
        if b == NB - 1:
            dqn[:, cols] = (dqT[h] * SCALE).astype(BF16).T

    def queries(half):
        arrived(2 + half)
        for h in range(half * 4, half * 4 + 4):
            qx[h, 0:HD, :] = qn[:, h * HD : h * HD + HD].T

    steps = [(b, h) for half in range(2) for b in (4, 3) for h in range(half * 4, half * 4 + 4)]
    steps += [(b, h) for b in (2, 1, 0) for h in range(GRP)]
    before = {
        (3, 0): lambda: relay(0, 2),
        (3, 3): lambda: (relay(1, 2), queries(1)),
        (4, 6): lambda: (prepare_keys(2), prepare_values(2)),
        (3, 4): lambda: relay(0, 1),
        (3, 6): lambda: relay(1, 1),
        (2, 5): lambda: (prepare_keys(1), prepare_values(1)),
        (1, 7): lambda: (relay(0, 0), prepare_keys(0)),
        (0, 0): lambda: (relay(1, 0), prepare_values(0)),
    }
    for n in range(2):
        arrived(n)
        hop(n, 4)
    prepare_keys(4)
    prepare_values(4)
    for n in range(2):
        relay(n, 3)
    prepare_keys(3)
    prepare_values(3)
    queries(0)
    tops = [None, None]
    for c in range(4):
        scores(4, 0, s_a, c, tops)
    put_tops(4, 0, tops)
    for i, (b, h) in enumerate(steps):
        if (b, h) in before:
            before[b, h]()
        now, later = (s_a, s_b) if i % 2 == 0 else (s_b, s_a)
        forward(b, h, now, later, steps[i + 1] if i + 1 < len(steps) else None)

    arrived(4)
    for h in range(GRP):
        gT[h] = gn[:, h * HD : h * HD + HD].T

    def finish(h, _):
        inv = 1.0 / sums[h, 0:1, :]
        o = (acc[h] * inv).astype(BF16)
        scal[h, NB : NB + 1, :] = jnp.sum(
            o.astype(F32) * gT[h].astype(F32), axis=0, keepdims=True
        )
        for b in range(NB):
            scal[h, b : b + 1, :] = (
                jnp.exp2((maxes[h, b : b + 1, :] - maxes[h, NB : NB + 1, :]) * LOG2) * inv
            )
        on[:, aligned(h, HD)] = o.T
        return 0

    lax.fori_loop(0, GRP, finish, 0, unroll=2)

    slab = aligned(x, wide)
    tail = []
    for r in (1, 3, 2):
        copy = remote(
            on.at[aligned(peer_x[r], SH), :], att.at[:, slab], o_send.at[r], o_recv.at[r], peers[r]
        )
        copy.start()
        tail.append(copy)
    own = pltpu.make_async_copy(on.at[mine, :], att.at[:, slab], loc.at[5])
    own.start()
    tail.append(own)

    reds = {}

    def pass_on(n, b):
        total = dkv[b % 2, n] * SCALE if n == 0 else dkv[b % 2, n]
        if b > 0:
            reds[n, b - 1].wait()
            total = total + ring_in[b - 1, n].astype(F32)
        ring_out[b, n] = total.astype(BF16)
        reds[n, b] = remote(
            ring_out.at[b, n], ring_in.at[b, n], red_send.at[n, b], red_recv.at[n, b], down
        )
        reds[n, b].start()

    def send_queries(h, heads, tag):
        here = pl.ds(h * HD, heads * HD)
        there = pl.ds(pl.multiple_of(x * wide + h * HD, HD), heads * HD)
        for r in (1, 3, 2):
            copy = remote(
                dqn.at[aligned(peer_x[r], SH), here], dq_out.at[:, there],
                dq_send.at[tag, r], dq_recv.at[tag, r], peers[r],
            )
            copy.start()
            tail.append(copy)
        own = pltpu.make_async_copy(dqn.at[mine, here], dq_out.at[:, there], dq_loc.at[tag])
        own.start()
        tail.append(own)

    def run(b, start, stop):
        into = dkv_own if b == NB - 1 else dkv.at[b % 2]

        def step(h, _):
            backward(b, h, into)
            return 0

        lax.fori_loop(start, stop, step, 0, unroll=4)

    zero = jnp.zeros((2, BLK, HD), F32)
    dkv[0] = zero
    dkv_own[...] = zero
    run(0, 0, GRP)
    pass_on(0, 0)
    pass_on(1, 0)
    dkv[1] = zero
    run(1, 0, GRP)
    pass_on(0, 1)
    dkv[0] = zero
    run(2, 0, 4)
    pass_on(1, 1)
    run(2, 4, GRP)
    pass_on(0, 2)
    dkv[1] = zero
    run(3, 0, 4)
    pass_on(1, 2)
    run(4, 0, 4)
    send_queries(0, 4, 0)
    run(3, 4, GRP)
    pass_on(0, 3)
    pass_on(1, 3)
    for h in range(4, GRP):
        backward(4, h, dkv_own)
        if h % 2:
            send_queries(h - 1, 2, h // 2 - 1)

    heads = aligned(x, HD)
    for n, out in enumerate((dk_out, dv_out)):
        total = dkv_own[n] * SCALE if n == 0 else dkv_own[n]
        reds[n, 3].wait()
        last[n] = (total + ring_in[3, n].astype(F32)).astype(BF16)
        for r in (1, 3, 2):
            copy = remote(
                last.at[n, aligned(peer_x[r], SH), :], out.at[:, heads],
                fin_send.at[n, r], fin_recv.at[n, r], peers[r],
            )
            copy.start()
            tail.append(copy)
        own = pltpu.make_async_copy(last.at[n, mine, :], out.at[:, heads], loc.at[8 + n])
        own.start()
        tail.append(own)
    for copy in tail:
        copy.wait()


def hand_on(*refs):
    done = refs[8]
    copies = [pltpu.make_async_copy(refs[n], refs[4 + n], done.at[n]) for n in range(4)]
    for copy in copies:
        copy.start()
    for copy in copies:
        copy.wait()


def per_device(query_rows, key_rows, value_rows, grad_out, doc_lengths):
    anywhere = pl.BlockSpec(memory_space=pl.ANY)
    dma = pltpu.SemaphoreType.DMA
    wide = GRP * HD
    shapes = [query_rows.shape, query_rows.shape, key_rows.shape, value_rows.shape]
    results = pl.pallas_call(
        kernel,
        out_shape=[pltpu.VMEM(s, BF16) for s in shapes],
        in_specs=[pl.BlockSpec(memory_space=pltpu.SMEM)] + [anywhere] * 4,
        out_specs=[pl.BlockSpec(memory_space=pltpu.VMEM)] * 4,
        scratch_shapes=[
            pltpu.VMEM((NB, BLK, HD), BF16),
            pltpu.VMEM((NB, BLK, HD), BF16),
            pltpu.VMEM((BLK, wide), BF16),
            pltpu.VMEM((BLK, wide), BF16),
            pltpu.VMEM((BLK, wide), BF16),
            pltpu.VMEM((BLK, wide), BF16),
            pltpu.VMEM((GRP, 2 * HD, BLK), BF16),
            pltpu.VMEM((GRP, HD, BLK), BF16),
            pltpu.VMEM((NB, BLK, 2 * HD), BF16),
            pltpu.VMEM((NB, HD, BLK), BF16),
            pltpu.VMEM((NB, HD + 16, BLK), BF16),
            pltpu.VMEM((GRP, NB, BLK, BLK), BF16),
            pltpu.VMEM((GRP, HD, BLK), F32),
            pltpu.VMEM((GRP, 8, BLK), F32),
            pltpu.VMEM((GRP, 8, BLK), F32),
            pltpu.VMEM((GRP, HD, BLK), F32),
            pltpu.VMEM((GRP, 8, BLK), F32),
            pltpu.VMEM((BLK, BLK), F32),
            pltpu.VMEM((BLK, BLK), F32),
            pltpu.VMEM((2, 2, BLK, HD), F32),
            pltpu.VMEM((2, BLK, HD), F32),
            pltpu.VMEM((4, 2, BLK, HD), BF16),
            pltpu.VMEM((4, 2, BLK, HD), BF16),
            pltpu.VMEM((2, BLK, HD), BF16),
            dma((5, 4)),
            dma((5, 4)),
            dma((10,)),
            dma((2, 5)),
            dma((2, 5)),
            dma((4,)),
            dma((4,)),
            dma((3, 4)),
            dma((3, 4)),
            dma((3,)),
            dma((2, 4)),
            dma((2, 4)),
            dma((2, 4)),
            dma((2, 4)),
        ],
        compiler_params=pltpu.CompilerParams(
            collective_id=0, has_side_effects=True, vmem_limit_bytes=60 * 1024 * 1024
        ),
    )(doc_lengths, query_rows, key_rows, value_rows, grad_out)
    return pl.pallas_call(
        hand_on,
        out_shape=[jax.ShapeDtypeStruct(s, BF16) for s in shapes],
        in_specs=[pl.BlockSpec(memory_space=pltpu.VMEM)] * 4,
        out_specs=[anywhere] * 4,
        scratch_shapes=[dma((4,))],
        compiler_params=pltpu.CompilerParams(vmem_limit_bytes=1024 * 1024),
    )(*results)


def solution(mesh):
    rows = P(("dp", "ulysses"), None)
    return jax.shard_map(
        per_device,
        mesh=mesh,
        in_specs=(rows, rows, rows, rows, P()),
        out_specs=(rows, rows, rows, rows),
        check_vma=False,
    )
```
